32 devices in a mesh: freq: 2 (over x), src: 16 (over z, y, core).
Axes of the slice: x: 2, y: 2, z: 4, core: 2. Of those that a mesh axis runs over, the one named last changes fastest.
Arguments:
- shots: bfloat16 [4, 8192, 8192], P('freq', 'src'), parts along dimension 0, may hold values from -6 to 6
- wavelet: float32 [4, 8192], P('freq', 'src'), parts along dimension 0, may hold values from -1.2 to 1.2
- obliquity: float32 [8192], P('src'), may hold values from 0.3 to 3
- aperture: int32 [64, 64, 4], P('src'), may hold values from -1 to 63, as said below
Outputs:
- multiples: bfloat16 [4, 8192, 8192], P('freq', None, 'src'), parts along dimension 0
The draws below stay inside these ranges and needn't reach their ends.
There are 2 independent parts, one for each index of `freq`. The reference program is written for one: setup_inputs(seed, part) draws one part's arguments, and reference() takes and returns one part's arrays. A program takes and returns all parts, laid end to end along the dimension named above; an argument that names none is the same for every part. Nothing has to cross between parts.
Inputs may be any that keep to these rules, and one draw needn't show every extreme that they name: `aperture`: entry (i, j, t) is -1 (unused) or a block k with |k - j| <= 2; no block stands twice in one list.
All inputs are finite; a program needn't handle non-finite values.
Results may differ from the reference program's by a relative error of at most 0.0072.
Values may be sent and summed in bfloat16 or wider, within the bound.
A program may use at most 192 MiB of HBM per device.

```python
import math
import jax
import jax.numpy as jnp
from jax import lax

N = 8192
BLK = 128
APW = 2
K_AP = 4
NB = 64


def draw_aperture(key, part):
    window_len = 2 * APW + 1
    scores = jax.random.randint(key, (NB, NB, window_len), 0, 1 << 20) * window_len + jnp.arange(window_len, dtype=jnp.int32)
    ordering = jnp.argsort(scores, axis=-1)[..., :K_AP].astype(jnp.int32)
    blocks = jnp.arange(NB, dtype=jnp.int32)[None, :, None] + ordering - APW
    dropped = jax.random.randint(jax.random.fold_in(key, 7), (NB, NB, K_AP), 0, 4)
    keeper = (blocks >= 0) & (blocks < NB) & ((dropped > 0) | (jnp.arange(K_AP)[None, None, :] == 0))
    return jnp.where(keeper, blocks, -1).astype(jnp.int32)


def level_of(key, dims, split, least, largest):
    def one(position, blocks):
        heights = jax.random.uniform(jax.random.fold_in(jax.random.fold_in(key, 6), position), (blocks,), jnp.float32, least / len(split), largest / len(split))
        return jnp.repeat(jnp.exp(heights), dims[position] // blocks).reshape((-1,) + (1,) * (len(dims) - position - 1))

    factor_of = one(*split[0])
    for cut in split[1:]:
        factor_of = factor_of * one(*cut)
    return factor_of


def scatter_about(own_key, shape, deviation, limit, cuts=(), held_as=jnp.bfloat16):
    result = jax.random.normal(own_key, shape, jnp.float32) * deviation
    if len(cuts) > 0:
        result = level_of(own_key, shape, cuts, -0.22, 0.18) * result
    return jnp.clip(result, min=-limit, max=limit).astype(held_as)


def setup_inputs(seed: int = 0, part: int = 0) -> dict:
    key_of = jax.random.split(jax.random.key(seed), 5)
    own_keys = jax.random.split(jax.random.fold_in(key_of[4], part), 5)
    return {
        "shots": scatter_about(own_keys[0], (2, N, N), 1.0, 6.0, ((1, 16),)),
        "wavelet": scatter_about(own_keys[1], (2, N), 0.2, 1.2, ((1, 16),), jnp.float32),
        "obliquity": jnp.clip(jnp.exp(math.log(3.0) - 2.3025851 * jax.random.uniform(key_of[2], (N,), jnp.float32) ** level_of(key_of[2], (N,), ((0, 16),), -0.2, 0.2)), 0.3, 3.0),
        "aperture": draw_aperture(jax.random.fold_in(key_of[4], 71), part),
    }


def complex_product(left_op, right_op):
    right_big = jnp.concatenate([jnp.concatenate([right_op[0], right_op[1]], axis=1), jnp.concatenate([-right_op[1], right_op[0]], axis=1)], axis=0)
    return -jnp.dot(left_op.astype(jnp.float32), right_big.astype(jnp.float32), preferred_element_type=jnp.float32, precision=lax.Precision.HIGHEST)


def reference(shots, wavelet, obliquity, aperture):
    shot_re = shots[0].astype(jnp.float32)
    shot_im = shots[1].astype(jnp.float32)
    wave_re = wavelet[0][:, None]
    wave_im = wavelet[1][:, None]
    scaled = jnp.stack([shot_re * wave_re - shot_im * wave_im, shot_re * wave_im + shot_im * wave_re]).astype(jnp.bfloat16)
    data = (scaled.astype(jnp.float32) * obliquity).astype(jnp.bfloat16)
    window_len = 2 * APW + 1
    rim_cols = APW * BLK
    colpad = jnp.pad(data, ((0, 0), (0, 0), (rim_cols, rim_cols)))
    rowpad = jnp.pad(data, ((0, 0), (rim_cols, rim_cols), (0, 0)))
    block_count = N // BLK

    def one_block(j):
        targets = j + jnp.arange(window_len, dtype=jnp.int32) - APW
        targets = jnp.where((targets >= 0) & (targets < block_count), targets, -2)
        lists = lax.dynamic_index_in_dim(aperture, j, 1, keepdims=False)
        block_mask = jnp.any(lists[:, :, None] == targets[None, None, :], axis=1)
        left_op = lax.dynamic_slice_in_dim(colpad, j * BLK, window_len * BLK, 2)
        left_op = left_op.reshape(2, block_count, BLK, window_len, BLK) * block_mask.astype(jnp.bfloat16)[None, :, None, :, None]
        left_op = jnp.concatenate([left_op[0].reshape(N, window_len * BLK), left_op[1].reshape(N, window_len * BLK)], axis=1)
        right_op = lax.dynamic_slice(rowpad, (jnp.int32(0), j * BLK, j * BLK), (2, window_len * BLK, BLK))
        return complex_product(left_op, right_op)

    results = lax.map(one_block, jnp.arange(block_count, dtype=jnp.int32))
    results = results.reshape(block_count, N, 2, BLK)
    results = jnp.transpose(results, (2, 1, 0, 3)).reshape(2, N, N)
    return results.astype(jnp.bfloat16)
```

```python
import functools

import jax
import jax.numpy as jnp
from jax import lax
from jax.experimental import pallas as pl
from jax.experimental.pallas import tpu as pltpu
from jax.sharding import PartitionSpec as P

BLK = 128
APW = 2
WIN = 2 * APW + 1
HALO = APW * BLK
SMALL_ROWS = 8
AHEAD = 4


def xor_index(index, d):
    bit, result = 1, index
    while bit <= d:
        if d & bit:
            result = result + bit - 2 * bit * ((index // bit) % 2)
        bit *= 2
    return result


def exchange_kernel(n, rows, width, shots, small, recv, small_all,
                    base_s, base_r, mate_s, mate_r, ext_s, ext_r, sm_s, sm_r, loc):
    me = lax.axis_index("src")
    half = n // 2
    odd = me % 2
    mate = xor_index(me, 1)

    def edge(t):
        return (t == 0) | (t == n - 1)

    def middle(t):
        return (t == half - 1) | (t == half)

    def rows_of(s, col, wide):
        return recv.at[:, pl.ds(pl.multiple_of(s * rows, rows), rows), pl.ds(pl.multiple_of(col, BLK), wide)]

    def cols_of(col, wide):
        return shots.at[:, :, pl.ds(pl.multiple_of(col, BLK), wide)]

    def remote(src, dst, send, got, t):
        return pltpu.make_async_remote_copy(
            src_ref=src, dst_ref=dst, send_sem=send, recv_sem=got,
            device_id={"src": t}, device_id_type=pl.DeviceIdType.MESH)

    def span(t, wide_case, both):
        t_odd = t % 2
        if both:
            if wide_case:
                return t * width - HALO, 0, width + 2 * HALO
            return t * width - HALO * t_odd, HALO * (1 - t_odd), width + HALO
        if wide_case:
            return t * width - HALO * (1 - t_odd), HALO * t_odd, width + HALO
        return t * width, HALO, width

    def wide_for(t, d):
        if d < half:
            return jnp.logical_not(edge(t))
        return middle(t)

    def both_ways(cond, act):
        @pl.when(cond)
        def _():
            act(True)

        @pl.when(jnp.logical_not(cond))
        def _():
            act(False)

    def outgoing(d, wide_case):
        t = xor_index(me, d)
        src_col, dst_col, wide = span(t, wide_case, d <= 1)
        return remote(cols_of(src_col, wide), rows_of(me, dst_col, wide), base_s.at[d], base_r.at[d], t)

    def incoming(d, wide_case):
        s = xor_index(me, d)
        _, dst_col, wide = span(me, wide_case, d <= 1)
        place = rows_of(s, dst_col, wide)
        return remote(place, place, base_s.at[d], base_r.at[d], s)

    def own_copy(wide_case):
        src_col, dst_col, wide = span(me, wide_case, True)
        return pltpu.make_async_copy(cols_of(src_col, wide), rows_of(me, dst_col, wide), loc.at[0])

    def mate_out(d):
        s = xor_index(me, d)
        src = rows_of(s, width * (1 - odd) + HALO * odd, HALO)
        return remote(src, rows_of(s, (HALO + width) * odd, HALO), mate_s.at[d], mate_r.at[d], mate)

    def mate_in(d):
        place = rows_of(xor_index(mate, d), (HALO + width) * (1 - odd), HALO)
        return remote(place, place, mate_s.at[d], mate_r.at[d], mate)

    neighbour = me - 1 + 2 * odd
    hands_on = jnp.logical_not(edge(me) | middle(me))

    def ext_out(d):
        s = xor_index(me, d)
        src = rows_of(s, HALO * (1 - odd) + width * odd, HALO)
        return remote(src, rows_of(s, (HALO + width) * (1 - odd), HALO), ext_s.at[d], ext_r.at[d], neighbour)

    def ext_in(d):
        place = rows_of(xor_index(neighbour, d), (HALO + width) * odd, HALO)
        return remote(place, place, ext_s.at[d], ext_r.at[d], neighbour)

    def small_out(d):
        return remote(small, small_all.at[me], sm_s.at[d], sm_r.at[d], xor_index(me, d))

    def small_in(d):
        place = small_all.at[xor_index(me, d)]
        return remote(place, place, sm_s.at[d], sm_r.at[d], xor_index(me, d))

    barrier = pltpu.get_barrier_semaphore()
    for d in range(1, n):
        pl.semaphore_signal(barrier, inc=1, device_id={"src": xor_index(me, d)},
                            device_id_type=pl.DeviceIdType.MESH)
    pl.semaphore_wait(barrier, n - 1)

    far = list(range(n - 1, half - 1, -1))
    near = list(range(half - 1, 0, -1))

    def sends(is_odd):
        return near + far if is_odd else far + near

    def arrivals(is_odd):
        place = {d: sends(bool(is_odd) != bool(d % 2)).index(d) for d in far + near}
        return sorted(far + near, key=lambda d: place[d])

    both_ways(jnp.logical_not(edge(me)), lambda w: own_copy(w).start())
    small_own = pltpu.make_async_copy(small, small_all.at[me], loc.at[1])
    small_own.start()
    for d in range(1, n):
        small_out(d).start()

    def run(is_odd):
        todo, come = sends(is_odd), arrivals(is_odd)
        for i in range(n - 1 + AHEAD):
            if i < n - 1:
                d = todo[i]
                both_ways(wide_for(xor_index(me, d), d), lambda w, d=d: outgoing(d, w).start())
            if i >= AHEAD:
                d = todo[i - AHEAD]
                both_ways(wide_for(xor_index(me, d), d), lambda w, d=d: outgoing(d, w).wait_send())
                d = come[i - AHEAD]
                both_ways(wide_for(me, d), lambda w, d=d: incoming(d, w).wait_recv())
                if d >= half:
                    @pl.when(hands_on)
                    def _(d=d):
                        ext_out(d).start()
                if d > 1:
                    mate_out(d).start()

    both_ways(odd == 1, run)

    for d in range(1, n):
        small_out(d).wait_send()
        small_in(d).wait_recv()
        if d > 1:
            mate_out(d).wait_send()
            mate_in(d).wait_recv()
        if d >= half:
            @pl.when(hands_on)
            def _(d=d):
                ext_out(d).wait_send()
                ext_in(d).wait_recv()
    both_ways(jnp.logical_not(edge(me)), lambda w: own_copy(w).wait())
    small_own.wait()


def product_kernel(rows, width, block_total, me_ref, aper, small, obl, recv, *rest):
    bands, out, rhs, left = rest[:-3], rest[-3], rest[-2], rest[-1]
    step = pl.program_id(0)
    me = me_ref[0]
    cols = width // BLK
    row_blocks = rows // BLK

    def make_data(block_ref, wave, start, wide):
        wave_re, wave_im = wave[:, 0:1], wave[:, 1:2]
        re = block_ref[0, :, start:start + wide].astype(jnp.float32)
        im = block_ref[1, :, start:start + wide].astype(jnp.float32)
        factor = obl[0:1, start:start + wide]
        s_re = (re * wave_re - im * wave_im).astype(jnp.bfloat16).astype(jnp.float32)
        s_im = (re * wave_im + im * wave_re).astype(jnp.bfloat16).astype(jnp.float32)
        return (s_re * factor).astype(jnp.bfloat16), (s_im * factor).astype(jnp.bfloat16)

    @pl.when(step == 0)
    def _():
        per = rows // HALO
        total = (block_total * BLK) // HALO
        for b, band in enumerate(bands):
            g = jnp.clip(me * (width // HALO) - 1 + b, 0, total - 1)
            lanes = pl.ds(pl.multiple_of((g % per) * HALO, BLK), HALO)
            wave = jnp.transpose(small[g // per, :, lanes])
            for j in range(cols):
                pair = [k for k in (APW * b, APW * b + 1) if 0 <= k - j < WIN]
                if not pair:
                    continue
                b_re, b_im = make_data(band, wave, HALO + j * BLK, BLK)
                for k in pair:
                    part = slice((k - APW * b) * BLK, (k - APW * b + 1) * BLK)
                    top = (k - j) * 2 * BLK
                    rhs[j, top:top + BLK, :BLK] = -b_re[part]
                    rhs[j, top:top + BLK, BLK:] = -b_im[part]
                    rhs[j, top + BLK:top + 2 * BLK, :BLK] = b_im[part]
                    rhs[j, top + BLK:top + 2 * BLK, BLK:] = -b_re[part]

    wave = jnp.transpose(small[step])
    for k in range(cols + 2 * APW):
        d_re, d_im = make_data(recv, wave, k * BLK, BLK)
        left[:, 2 * k * BLK:(2 * k + 1) * BLK] = d_re
        left[:, (2 * k + 1) * BLK:(2 * k + 2) * BLK] = d_im

    for j in range(cols):
        strips = []
        for r in range(row_blocks):
            listed = [aper[step * row_blocks + r, j * aper.shape[1] // cols + t] for t in range(aper.shape[1] // cols)]
            pieces = []
            for w in range(WIN):
                k = me * cols + j + w - APW
                hit = listed[0] == k
                for entry in listed[1:]:
                    hit = hit | (entry == k)
                hit = hit & (k >= 0) & (k < block_total)
                piece = left[r * BLK:(r + 1) * BLK, (j + w) * 2 * BLK:(j + w + 1) * 2 * BLK]
                pieces.append(jnp.where(hit, piece, jnp.zeros_like(piece)))
            strips.append(jnp.concatenate(pieces, axis=1))
        product = jnp.dot(jnp.concatenate(strips, axis=0), rhs[j], preferred_element_type=jnp.float32)
        out[0, :, j * BLK:(j + 1) * BLK] = product[:, :BLK].astype(jnp.bfloat16)
        out[1, :, j * BLK:(j + 1) * BLK] = product[:, BLK:].astype(jnp.bfloat16)


def per_device(n, shots, wavelet, obliquity, aperture):
    rows, total = shots.shape[1], shots.shape[2]
    width = total // n
    block_total = total // BLK
    row_blocks, _, entries = aperture.shape
    cols = width // BLK
    spread = width + 2 * HALO
    me = lax.axis_index("src")
    aper_rows = row_blocks * block_total * entries // rows
    small = jnp.concatenate([
        wavelet,
        obliquity[None, :],
        aperture.astype(jnp.float32).reshape(aper_rows, rows),
        jnp.zeros((SMALL_ROWS - 3 - aper_rows, rows), jnp.float32),
    ])
    anywhere = pl.BlockSpec(memory_space=pl.ANY)
    recv, small_all = pl.pallas_call(
        functools.partial(exchange_kernel, n, rows, width),
        out_shape=(
            jax.ShapeDtypeStruct((2, total, spread), shots.dtype),
            jax.ShapeDtypeStruct((n, SMALL_ROWS, rows), jnp.float32),
        ),
        in_specs=[anywhere, anywhere],
        out_specs=(anywhere, anywhere),
        scratch_shapes=[pltpu.SemaphoreType.DMA((n,))] * 8 + [pltpu.SemaphoreType.DMA((2,))],
        compiler_params=pltpu.CompilerParams(collective_id=0, has_side_effects=True),
    )(shots, small)

    aper = small_all[:, 3:3 + aper_rows].astype(jnp.int32).reshape(block_total, block_total * entries)
    aper = lax.dynamic_slice(aper, (jnp.int32(0), me * cols * entries), (block_total, cols * entries))
    before = lax.dynamic_slice(small_all, (jnp.maximum(me - 1, 0), 2, rows - HALO), (1, 1, HALO))
    after = lax.dynamic_slice(small_all, (jnp.minimum(me + 1, n - 1), 2, 0), (1, 1, HALO))
    obl = jnp.concatenate([before[0, 0], obliquity, after[0, 0]])[None, :]

    band_count = width // HALO + 2
    band_total = total // HALO


    return pl.pallas_call(
        functools.partial(product_kernel, rows, width, block_total),
        grid_spec=pltpu.PrefetchScalarGridSpec(
            num_scalar_prefetch=2,
            grid=(n,),
            in_specs=[
                pl.BlockSpec((n, SMALL_ROWS, rows), lambda i, *_: (0, 0, 0)),
                pl.BlockSpec((1, spread), lambda i, *_: (0, 0)),
                pl.BlockSpec((2, rows, spread), lambda i, *_: (0, i, 0)),
            ] + [
                pl.BlockSpec(
                    (2, HALO, spread),
                    lambda i, me_ref, aper_ref, b=b: (
                        0, jnp.clip(me_ref[0] * (width // HALO) - 1 + b, 0, band_total - 1), 0))
                for b in range(band_count)
            ],
            out_specs=pl.BlockSpec((2, rows, width), lambda i, *_: (0, i, 0)),
            scratch_shapes=[
                pltpu.VMEM((cols, WIN * 2 * BLK, 2 * BLK), jnp.bfloat16),
                pltpu.VMEM((rows, (cols + 2 * APW) * 2 * BLK), jnp.bfloat16),
            ],
        ),
        out_shape=jax.ShapeDtypeStruct((2, total, width), jnp.bfloat16),
        compiler_params=pltpu.CompilerParams(vmem_limit_bytes=48 * 1024 * 1024),
    )(me[None], aper, small_all, obl, recv, *([recv] * band_count))


def solution(mesh):
    return jax.shard_map(
        functools.partial(per_device, mesh.shape["src"]),
        mesh=mesh,
        in_specs=(P("freq", "src", None), P("freq", "src"), P("src"), P("src", None, None)),
        out_specs=P("freq", None, "src"),
        check_vma=False,
    )
```

```python
import functools

import jax
import jax.numpy as jnp
from jax import lax
from jax.experimental import pallas as pl
from jax.experimental.pallas import tpu as pltpu
from jax.sharding import PartitionSpec as P

BLK = 128
APW = 2
WIN = 2 * APW + 1
HALO = APW * BLK
MOST_PARTS = 2
AHEAD = 8
SLACK = 2
NEAR_SHARE = 1.0
NEAR_FIRST = 0


def xor_index(index, d):
    bit, result = 1, index
    while bit <= d:
        if d & bit:
            result = result + bit - 2 * bit * ((index // bit) % 2)
        bit *= 2
    return result


def xor_traced(a, b, n):
    bit, result = 1, 0
    while bit < n:
        result = result + bit * ((a // bit + b // bit) % 2)
        bit *= 2
    return result


def pick(index, table):
    result = jnp.int32(0)
    for i, value in enumerate(table):
        result = result + jnp.where(index == i, value, 0)
    return result


def high_bit(d):
    return 1 << (d.bit_length() - 1)


def merge(a, b, share):
    out, i, j = [], 0, 0
    while i < len(a) or j < len(b):
        if j == len(b) or (i < len(a) and (i + 1) * len(b) <= (j + 1) * share * len(a)):
            out.append(a[i])
            i += 1
        else:
            out.append(b[j])
            j += 1
    return out


def make_plan(n, inner, parts):
    half = n // 2
    near_pairs = [0] + list(range(half - 2, 1, -2))
    far_pairs = list(range(n - 2, half - 1, -2))

    def pieces(kind, pairs):
        return [(kind, d + 1 - u, h) for d in pairs for h in range(parts) for u in range(2) if d + 1 - u]

    far = pieces("edge", far_pairs) + (pieces("inner", far_pairs) if inner else [])
    near = pieces("near", near_pairs)
    order = near[:NEAR_FIRST] + merge(far, near[NEAR_FIRST:], NEAR_SHARE)
    at = {piece: i for i, piece in enumerate(order)}
    items = []
    for d in near_pairs + far_pairs:
        for h in range(parts):
            if d < half:
                needs = [("near", e, h) for e in (d, d + 1) if e]
                kind = "near"
            else:
                needs = [("edge", e, h) for e in (d, d + 1)]
                needs += [("inner", e, h) for e in (d, d + 1)] if inner else []
                kind = "edge"
            x = 3
            while d and x < high_bit(d):
                needs += [(kind, e ^ x, h) for e in (d, d + 1)]
                x = 2 * x + 1
            if d == 0:
                needs += [("near", 1, e) for e in range(parts)] + [("edge", n - 1, e) for e in range(parts)]
            items.append((max(at[p] for p in needs), d, h))
    items.sort()
    return order, items


def kernel(n, rows, width, shots, wave, obl, aper, out,
           recv, band, rhs, left, wave_all, obl_win, aper_all, aper_s,
           base_s, base_r, in_s, in_r, band_s, band_r, mate_s, mate_r, ext_s, ext_r,
           wave_ss, wave_sr, aper_ss, aper_sr, obl_ss, obl_sr, loc):
    parts = min(MOST_PARTS, rows // BLK)
    me = lax.axis_index("src")
    half = n // 2
    odd = me % 2
    mate = xor_index(me, 1)
    neighbour = me - 1 + 2 * odd
    total = n * rows
    block_total = total // BLK
    cols = width // BLK
    part_rows = rows // parts
    inner = width - HALO
    entries = aper.shape[1]

    def edge(t):
        return (t == 0) | (t == n - 1)

    def middle(t):
        return (t == half - 1) | (t == half)

    inside = jnp.logical_not(edge(me))

    def handed(t, d):
        high = high_bit(d)
        if high < 4:
            return False
        return (t + t % 2) % high != 0

    def direct(t, d):
        if handed(t, d) is False:
            return jnp.logical_not(edge(t))
        return jnp.logical_not(edge(t) | handed(t, d))

    def lanes(col, wide):
        return pl.ds(pl.multiple_of(col, BLK), wide)

    def rows_of(s, col, wide, h):
        return recv.at[:, pl.ds(pl.multiple_of(s * rows + h * part_rows, BLK), part_rows), lanes(col, wide)]

    def cols_of(col, wide, h):
        return shots.at[:, pl.ds(h * part_rows, part_rows), lanes(col, wide)]

    def remote(src, dst, send, got, t):
        return pltpu.make_async_remote_copy(
            src_ref=src, dst_ref=dst, send_sem=send, recv_sem=got,
            device_id={"src": t}, device_id_type=pl.DeviceIdType.MESH)

    def both_ways(cond, act):
        @pl.when(cond)
        def _():
            act(True)

        @pl.when(jnp.logical_not(cond))
        def _():
            act(False)

    def span(t, d, wide_case):
        t_odd = t % 2
        if d <= 1:
            if wide_case:
                return t * width - HALO, 0, width + 2 * HALO
            return t * width - HALO * t_odd, HALO * (1 - t_odd), width + HALO
        if d < half:
            if wide_case:
                return t * width - HALO * (1 - t_odd), HALO * t_odd, width + HALO
            return t * width, HALO, width
        if wide_case:
            return t * width + (width - HALO) * t_odd - HALO * (1 - t_odd), width * t_odd, 2 * HALO
        return t * width + (width - HALO) * t_odd, HALO + (width - HALO) * t_odd, HALO

    def base_out(d, h, wide_case):
        t = xor_index(me, d)
        i = d * parts + h
        src_col, dst_col, wide = span(t, d, wide_case)
        return remote(cols_of(src_col, wide, h), rows_of(me, dst_col, wide, h), base_s.at[i], base_r.at[i], t)

    def base_in(d, h, wide_case):
        s = xor_index(me, d)
        i = d * parts + h
        _, dst_col, wide = span(me, d, wide_case)
        place = rows_of(s, dst_col, wide, h)
        return remote(place, place, base_s.at[i], base_r.at[i], s)

    def own_copy(h, wide_case):
        src_col, dst_col, wide = span(me, 0, wide_case)
        return pltpu.make_async_copy(cols_of(src_col, wide, h), rows_of(me, dst_col, wide, h), loc.at[5 + h])

    def inner_out(d, h):
        t = xor_index(me, d)
        i = (d - half) * parts + h
        return remote(cols_of(t * width + HALO * (1 - t % 2), inner, h), rows_of(me, HALO + HALO * (1 - t % 2), inner, h),
                      in_s.at[i], in_r.at[i], t)

    def inner_in(d, h):
        s = xor_index(me, d)
        i = (d - half) * parts + h
        place = rows_of(s, HALO + HALO * (1 - odd), inner, h)
        return remote(place, place, in_s.at[i], in_r.at[i], s)

    def mate_out(d, h):
        i = d * parts + h
        s = xor_index(me, d)
        return remote(rows_of(s, width * (1 - odd) + HALO * odd, HALO, h), rows_of(s, (HALO + width) * odd, HALO, h),
                      mate_s.at[i], mate_r.at[i], mate)

    def mate_in(d, h):
        i = d * parts + h
        place = rows_of(xor_index(mate, d), (HALO + width) * (1 - odd), HALO, h)
        return remote(place, place, mate_s.at[i], mate_r.at[i], mate)

    def ext_out(d, h):
        i = (d - 4) * parts + h
        s = xor_index(me, d)
        return remote(rows_of(s, HALO * (1 - odd) + width * odd, HALO, h), rows_of(s, (HALO + width) * (1 - odd), HALO, h),
                      ext_s.at[i], ext_r.at[i], neighbour)

    def ext_in(d, h):
        i = (d - 4) * parts + h
        place = rows_of(xor_index(neighbour, d), (HALO + width) * odd, HALO, h)
        return remote(place, place, ext_s.at[i], ext_r.at[i], neighbour)

    banded = jnp.logical_not(edge(me) | middle(me))

    def band_out():
        src = shots.at[:, pl.ds(pl.multiple_of((rows - HALO) * odd, HALO), HALO),
                       lanes(neighbour * width + (width - HALO) * (1 - odd), HALO)]
        return remote(src, band, band_s, band_r, neighbour)

    def band_in():
        return remote(band, band, band_s, band_r, neighbour)

    def small_ends(d, device):
        if d <= half:
            return device, xor_index(device, d)
        return xor_index(device, half), xor_index(device, d - half)

    def smalls_out(d):
        slot, t = small_ends(d, me)
        first = d <= half
        return (
            remote(wave if first else wave_all.at[slot], wave_all.at[slot], wave_ss.at[d], wave_sr.at[d], t),
            remote(aper if first else aper_all.at[slot], aper_all.at[slot], aper_ss.at[d], aper_sr.at[d], t),
        )

    def smalls_in(d):
        sender = xor_index(me, d if d <= half else d - half)
        slot, _ = small_ends(d, sender)
        return (
            remote(wave_all.at[slot], wave_all.at[slot], wave_ss.at[d], wave_sr.at[d], sender),
            remote(aper_all.at[slot], aper_all.at[slot], aper_ss.at[d], aper_sr.at[d], sender),
        )

    def obl_left():
        return remote(obl.at[:, 0:HALO], obl_win.at[:, HALO + width:HALO + width + HALO], obl_ss.at[0], obl_sr.at[0], me - 1)

    def obl_right():
        return remote(obl.at[:, width - HALO:width], obl_win.at[:, 0:HALO], obl_ss.at[1], obl_sr.at[1], me + 1)

    def own_smalls():
        return (
            pltpu.make_async_copy(wave, wave_all.at[me], loc.at[1]),
            pltpu.make_async_copy(aper, aper_all.at[me], loc.at[2]),
            pltpu.make_async_copy(obl, obl_win.at[:, HALO:HALO + width], loc.at[3]),
        )

    def to_scalar():
        return pltpu.make_async_copy(aper_all, aper_s, loc.at[4])

    barrier = pltpu.get_barrier_semaphore()
    for d in range(1, n):
        pl.semaphore_signal(barrier, inc=1, device_id={"src": xor_index(me, d)},
                            device_id_type=pl.DeviceIdType.MESH)
    pl.semaphore_wait(barrier, n - 1)

    order, items = make_plan(n, inner, parts)
    state = {"started": 0, "done": 0, "ext": set(), "mate": set()}

    def piece_act(piece, sending, act):
        kind, d, h = piece
        if kind == "inner":
            act(inner_out(d, h) if sending else inner_in(d, h))
        elif sending:
            both_ways(direct(xor_index(me, d), d), lambda w: act(base_out(d, h, w)))
        else:
            both_ways(direct(me, d), lambda w: act(base_in(d, h, w)))

    def size(piece):
        return 2 if piece[0] == "near" else 1

    def fill():
        while state["started"] < len(order) and (
                sum(size(p) for p in order[state["done"]:state["started"] + 1]) <= AHEAD):
            piece_act(order[state["started"]], True, lambda copy: copy.start())
            state["started"] += 1

    def pump():
        piece = order[state["done"]]
        piece_act(piece, True, lambda copy: copy.wait_send())
        state["done"] += 1
        fill()
        piece_act(piece, False, lambda copy: copy.wait_recv())
        kind, d, h = piece
        if kind != "inner" and handed(me, d) is not False:
            @pl.when(inside & handed(me, d))
            def _():
                ext_out(d, h).start()
        if d > 1 and (kind != "edge" or not inner):
            mate_out(d, h).start()

    def ready(d, h):
        if d == 0:
            if "own" not in state:
                state["own"] = True
                for part in range(parts):
                    both_ways(jnp.logical_not(edge(me)), lambda w: own_copy(part, w).wait())
            return
        for e in (d + 1, d):
            mate_in(e, h).wait_recv()
        if high_bit(d) >= 4:
            high = high_bit(d)
            group = [e for e in range(high, 2 * high) if (e, h) not in state["ext"]]
            if group:
                @pl.when(inside & handed(me, d))
                def _():
                    for e in group:
                        ext_in(e, h).wait_recv()
                state["ext"] |= {(e, h) for e in group}

    def smalls_ready():
        for d in range(1, n):
            if d != half:
                for copy in smalls_in(d):
                    copy.wait_recv()
        for copy in own_smalls():
            copy.wait()

        @pl.when(me > 0)
        def _():
            obl_right().wait_recv()

        @pl.when(me < n - 1)
        def _():
            obl_left().wait_recv()
        to_scalar().start()
        to_scalar().wait()

    def forward_smalls():
        for copy in smalls_in(half):
            copy.wait_recv()
        for d in range(half + 1, n):
            for copy in smalls_out(d):
                copy.start()

    def make_data(re, im, wave_re, wave_im, factor):
        re, im = re.astype(jnp.float32), im.astype(jnp.float32)
        s_re = (re * wave_re - im * wave_im).astype(jnp.bfloat16).astype(jnp.float32)
        s_im = (re * wave_im + im * wave_re).astype(jnp.bfloat16).astype(jnp.float32)
        return (s_re * factor).astype(jnp.bfloat16), (s_im * factor).astype(jnp.bfloat16)

    def wave_columns(s, row, count):
        part = wave_all[s, :, pl.ds(pl.multiple_of(row, BLK), count)]
        part = jnp.concatenate([part, jnp.zeros((6, count), jnp.float32)])
        part = jnp.transpose(part)
        return part[:, 0:1], part[:, 1:2]

    def build_rhs():
        for b in range(width // HALO + 2):
            g = jnp.clip(me * (width // HALO) - 1 + b, 0, total // HALO - 1)
            outer = b in (0, width // HALO + 1)
            other = odd == (1 if b else 0)
            row = pl.multiple_of(jnp.where(other, me * rows, g * HALO) if outer else g * HALO, HALO)
            wave_re, wave_im = wave_columns(g // (rows // HALO), (g % (rows // HALO)) * HALO, HALO)
            for j in range(cols):
                pair = [k for k in (APW * b, APW * b + 1) if 0 <= k - j < WIN]
                if not pair:
                    continue
                at = slice(HALO + j * BLK, HALO + (j + 1) * BLK)
                re, im = recv[0, pl.ds(row, HALO), at], recv[1, pl.ds(row, HALO), at]
                first = j * BLK - (width - HALO if b else 0)
                if outer and 0 <= first < HALO:
                    re = jnp.where(other, band[0, :, first:first + BLK], re)
                    im = jnp.where(other, band[1, :, first:first + BLK], im)
                b_re, b_im = make_data(re, im, wave_re, wave_im, obl_win[0:1, at])
                for k in pair:
                    part = slice((k - APW * b) * BLK, (k - APW * b + 1) * BLK)
                    top = (k - j) * 2 * BLK
                    rhs[j, top:top + BLK, :BLK] = -b_re[part]
                    rhs[j, top:top + BLK, BLK:] = -b_im[part]
                    rhs[j, top + BLK:top + 2 * BLK, :BLK] = b_im[part]
                    rhs[j, top + BLK:top + 2 * BLK, BLK:] = -b_re[part]

    def multiply(s, h):
        first = pl.multiple_of(s * rows + h * part_rows, BLK)
        here = pl.ds(first, part_rows)
        wave_re, wave_im = wave_columns(s, h * part_rows, part_rows)
        for k in range(cols + 2 * APW):
            at = slice(k * BLK, (k + 1) * BLK)
            d_re, d_im = make_data(recv[0, here, at], recv[1, here, at], wave_re, wave_im, obl_win[0:1, at])
            left[:, 2 * k * BLK:(2 * k + 1) * BLK] = d_re
            left[:, (2 * k + 1) * BLK:(2 * k + 2) * BLK] = d_im
        for j in range(cols):
            strips = []
            for r in range(part_rows // BLK):
                listed = [aper_s[s, h * (part_rows // BLK) + r, t, me * cols + j] for t in range(entries)]
                blocks = []
                for w in range(WIN):
                    k = me * cols + j + w - APW
                    hit = listed[0] == k
                    for entry in listed[1:]:
                        hit = hit | (entry == k)
                    hit = hit & (k >= 0) & (k < block_total)
                    block = left[r * BLK:(r + 1) * BLK, (j + w) * 2 * BLK:(j + w + 1) * 2 * BLK]
                    blocks.append(jnp.where(hit, block, jnp.zeros_like(block)))
                strips.append(jnp.concatenate(blocks, axis=1))
            product = jnp.dot(jnp.concatenate(strips, axis=0), rhs[j], preferred_element_type=jnp.float32)
            out[0, here, j * BLK:(j + 1) * BLK] = product[:, :BLK].astype(jnp.bfloat16)
            out[1, here, j * BLK:(j + 1) * BLK] = product[:, BLK:].astype(jnp.bfloat16)

    @pl.when(banded)
    def _():
        band_out().start()
    fill()
    for h in range(parts):
        both_ways(jnp.logical_not(edge(me)), lambda w: own_copy(h, w).start())
    for d in list(range(half, 0, -1)):
        for copy in smalls_out(d):
            copy.start()

    @pl.when(me > 0)
    def _():
        obl_left().start()

    @pl.when(me < n - 1)
    def _():
        obl_right().start()
    for copy in own_smalls():
        copy.start()
    forward_smalls()

    def item(step, carry):
        for index, (last, d, h) in enumerate(items):
            @pl.when(step == 2 * index)
            def _(last=last, d=d, h=h, index=index):
                upto = len(order) if index == len(items) - 1 else min(last + 1 + SLACK, len(order))
                while state["done"] < upto:
                    pump()
                ready(d, h)
                if index == 0:
                    for other in range(1, parts):
                        if ("near", 0, other) not in state["mate"]:
                            pass
                    smalls_ready()

                    @pl.when(banded)
                    def _():
                        band_in().wait_recv()

                    @pl.when(jnp.logical_not(banded))
                    def _():
                        row = jnp.clip(me * rows - HALO + (rows + HALO) * odd, 0, total - HALO)
                        band[...] = recv[:, pl.ds(pl.multiple_of(row, HALO), HALO), lanes(HALO + (width - HALO) * odd, HALO)]
                    build_rhs()

        q = step // 2
        d = pick(q, [d for _, d, _ in items]) + 1 - step % 2
        multiply(xor_traced(me, d, n), pick(q, [h for _, _, h in items]))
        return carry

    lax.fori_loop(0, 2 * len(items), item, 0)

    for d in range(1, n):
        for copy in smalls_out(d):
            copy.wait_send()
        for h in range(parts):
            if d > 1:
                mate_out(d, h).wait_send()
            if handed(me, d) is not False:
                @pl.when(inside & handed(me, d))
                def _(d=d, h=h):
                    ext_out(d, h).wait_send()

    @pl.when(banded)
    def _():
        band_out().wait_send()

    @pl.when(me > 0)
    def _():
        obl_left().wait_send()

    @pl.when(me < n - 1)
    def _():
        obl_right().wait_send()


def per_device(n, shots, wavelet, obliquity, aperture):
    rows, total = shots.shape[1], shots.shape[2]
    width = total // n
    cols = width // BLK
    half = n // 2
    parts = min(MOST_PARTS, rows // BLK)
    spread = width + 2 * HALO
    aper = jnp.transpose(aperture, (0, 2, 1))
    anywhere = pl.BlockSpec(memory_space=pl.ANY)
    dma = pltpu.SemaphoreType.DMA
    return pl.pallas_call(
        functools.partial(kernel, n, rows, width),
        out_shape=pltpu.VMEM((2, total, width), jnp.bfloat16),
        in_specs=[anywhere] * 4,
        out_specs=pl.BlockSpec(memory_space=pltpu.VMEM),
        scratch_shapes=[
            pltpu.VMEM((2, total, spread), jnp.bfloat16),
            pltpu.VMEM((2, HALO, HALO), jnp.bfloat16),
            pltpu.VMEM((cols, WIN * 2 * BLK, 2 * BLK), jnp.bfloat16),
            pltpu.VMEM((rows // parts, (cols + 2 * APW) * 2 * BLK), jnp.bfloat16),
            pltpu.VMEM((n,) + wavelet.shape, jnp.float32),
            pltpu.VMEM((1, spread), jnp.float32),
            pltpu.VMEM((n,) + aper.shape, jnp.int32),
            pltpu.SMEM((n,) + aper.shape, jnp.int32),
            dma((n * parts,)), dma((n * parts,)), dma((half * parts,)), dma((half * parts,)), dma, dma,
            dma((n * parts,)), dma((n * parts,)), dma(((n - 4) * parts,)), dma(((n - 4) * parts,)),
            dma((n,)), dma((n,)), dma((n,)), dma((n,)), dma((2,)), dma((2,)), dma((5 + parts,)),
        ],
        compiler_params=pltpu.CompilerParams(
            collective_id=0, has_side_effects=True, vmem_limit_bytes=42 * 1024 * 1024),
    )(shots, wavelet, obliquity[None, :], aper)


def solution(mesh):
    return jax.shard_map(
        functools.partial(per_device, mesh.shape["src"]),
        mesh=mesh,
        in_specs=(P("freq", "src", None), P("freq", "src"), P("src"), P("src", None, None)),
        out_specs=P("freq", None, "src"),
        check_vma=False,
    )
```

```python
import functools

import jax
import jax.numpy as jnp
from jax import lax
from jax.experimental import pallas as pl
from jax.experimental.pallas import tpu as pltpu
from jax.sharding import PartitionSpec as P

BLK = 128
APW = 2
WIN = 2 * APW + 1
HALO = APW * BLK
MOST_PARTS = 2
AHEAD = 9
SLACK = 2


def xor_index(index, d):
    bit, result = 1, index
    while bit <= d:
        if d & bit:
            result = result + bit - 2 * bit * ((index // bit) % 2)
        bit *= 2
    return result


def xor_traced(a, b, n):
    bit, result = 1, 0
    while bit < n:
        result = result + bit * ((a // bit + b // bit) % 2)
        bit *= 2
    return result


def pick(index, table):
    result = jnp.int32(0)
    for i, value in enumerate(table):
        result = result + jnp.where(index == i, value, 0)
    return result


def high_bit(d):
    return 1 << (d.bit_length() - 1)


def merge(a, b):
    out, i, j = [], 0, 0
    while i < len(a) or j < len(b):
        if j == len(b) or (i < len(a) and (i + 1) * len(b) <= (j + 1) * len(a)):
            out.append(a[i])
            i += 1
        else:
            out.append(b[j])
            j += 1
    return out


def make_plan(n, inner, parts):
    half = n // 2
    near_pairs = [0] + list(range(half - 2, 1, -2))
    far_pairs = list(range(n - 2, half - 1, -2))

    def pieces(kind, pairs):
        return [(kind, d + 1 - u, h) for d in pairs for h in range(parts) for u in range(2) if d + 1 - u]

    far = pieces("edge", far_pairs) + (pieces("inner", far_pairs) if inner else [])
    near = pieces("near", near_pairs)
    order = near[:parts] + merge(far, near[parts:])
    at = {piece: i for i, piece in enumerate(order)}
    items = []
    for d in near_pairs + far_pairs:
        for h in range(parts):
            if d < half:
                needs = [("near", e, h) for e in (d, d + 1) if e]
                kind = "near"
            else:
                needs = [("edge", e, h) for e in (d, d + 1)]
                needs += [("inner", e, h) for e in (d, d + 1)] if inner else []
                kind = "edge"
            x = 3
            while d and x < high_bit(d):
                needs += [(kind, e ^ x, h) for e in (d, d + 1)]
                x = 2 * x + 1
            if d == 0:
                needs += [("near", 1, e) for e in range(parts)] + [("edge", n - 1, e) for e in range(parts)]
            items.append((max(at[p] for p in needs), d, h))
    items.sort()
    return order, items


def kernel(n, rows, width, shots, wave, obl, aper, out,
           recv, band, rhs, left, wave_all, obl_win, aper_all, aper_s,
           base_s, base_r, in_s, in_r, band_s, band_r, mate_s, mate_r, ext_s, ext_r,
           wave_ss, wave_sr, aper_ss, aper_sr, obl_ss, obl_sr, loc):
    parts = min(MOST_PARTS, rows // BLK)
    me = lax.axis_index("src")
    half = n // 2
    odd = me % 2
    mate = xor_index(me, 1)
    neighbour = me - 1 + 2 * odd
    total = n * rows
    block_total = total // BLK
    cols = width // BLK
    part_rows = rows // parts
    inner = width - HALO
    entries = aper.shape[1]

    def edge(t):
        return (t == 0) | (t == n - 1)

    def middle(t):
        return (t == half - 1) | (t == half)

    inside = jnp.logical_not(edge(me))

    def handed(t, d):
        high = high_bit(d)
        if high < 4:
            return False
        return (t + t % 2) % high != 0

    def direct(t, d):
        if handed(t, d) is False:
            return jnp.logical_not(edge(t))
        return jnp.logical_not(edge(t) | handed(t, d))

    def lanes(col, wide):
        return pl.ds(pl.multiple_of(col, BLK), wide)

    def rows_of(s, col, wide, h):
        return recv.at[:, pl.ds(pl.multiple_of(s * rows + h * part_rows, BLK), part_rows), lanes(col, wide)]

    def cols_of(col, wide, h):
        return shots.at[:, pl.ds(h * part_rows, part_rows), lanes(col, wide)]

    def remote(src, dst, send, got, t):
        return pltpu.make_async_remote_copy(
            src_ref=src, dst_ref=dst, send_sem=send, recv_sem=got,
            device_id={"src": t}, device_id_type=pl.DeviceIdType.MESH)

    def both_ways(cond, act):
        @pl.when(cond)
        def _():
            act(True)

        @pl.when(jnp.logical_not(cond))
        def _():
            act(False)

    def span(t, d, wide_case):
        t_odd = t % 2
        if d <= 1:
            if wide_case:
                return t * width - HALO, 0, width + 2 * HALO
            return t * width - HALO * t_odd, HALO * (1 - t_odd), width + HALO
        if d < half:
            if wide_case:
                return t * width - HALO * (1 - t_odd), HALO * t_odd, width + HALO
            return t * width, HALO, width
        if wide_case:
            return t * width + (width - HALO) * t_odd - HALO * (1 - t_odd), width * t_odd, 2 * HALO
        return t * width + (width - HALO) * t_odd, HALO + (width - HALO) * t_odd, HALO

    def base_out(d, h, wide_case):
        t = xor_index(me, d)
        i = d * parts + h
        src_col, dst_col, wide = span(t, d, wide_case)
        return remote(cols_of(src_col, wide, h), rows_of(me, dst_col, wide, h), base_s.at[i], base_r.at[i], t)

    def base_in(d, h, wide_case):
        s = xor_index(me, d)
        i = d * parts + h
        _, dst_col, wide = span(me, d, wide_case)
        place = rows_of(s, dst_col, wide, h)
        return remote(place, place, base_s.at[i], base_r.at[i], s)

    def own_copy(h, wide_case):
        src_col, dst_col, wide = span(me, 0, wide_case)
        return pltpu.make_async_copy(cols_of(src_col, wide, h), rows_of(me, dst_col, wide, h), loc.at[5 + h])

    def inner_out(d, h):
        t = xor_index(me, d)
        i = (d - half) * parts + h
        return remote(cols_of(t * width + HALO * (1 - t % 2), inner, h), rows_of(me, HALO + HALO * (1 - t % 2), inner, h),
                      in_s.at[i], in_r.at[i], t)

    def inner_in(d, h):
        s = xor_index(me, d)
        i = (d - half) * parts + h
        place = rows_of(s, HALO + HALO * (1 - odd), inner, h)
        return remote(place, place, in_s.at[i], in_r.at[i], s)

    def mate_out(d, h):
        i = d * parts + h
        s = xor_index(me, d)
        return remote(rows_of(s, width * (1 - odd) + HALO * odd, HALO, h), rows_of(s, (HALO + width) * odd, HALO, h),
                      mate_s.at[i], mate_r.at[i], mate)

    def mate_in(d, h):
        i = d * parts + h
        place = rows_of(xor_index(mate, d), (HALO + width) * (1 - odd), HALO, h)
        return remote(place, place, mate_s.at[i], mate_r.at[i], mate)

    def ext_out(d, h):
        i = (d - 4) * parts + h
        s = xor_index(me, d)
        return remote(rows_of(s, HALO * (1 - odd) + width * odd, HALO, h), rows_of(s, (HALO + width) * (1 - odd), HALO, h),
                      ext_s.at[i], ext_r.at[i], neighbour)

    def ext_in(d, h):
        i = (d - 4) * parts + h
        place = rows_of(xor_index(neighbour, d), (HALO + width) * odd, HALO, h)
        return remote(place, place, ext_s.at[i], ext_r.at[i], neighbour)

    banded = jnp.logical_not(edge(me) | middle(me))

    def band_out():
        src = shots.at[:, pl.ds(pl.multiple_of((rows - HALO) * odd, HALO), HALO),
                       lanes(neighbour * width + (width - HALO) * (1 - odd), HALO)]
        return remote(src, band, band_s, band_r, neighbour)

    def band_in():
        return remote(band, band, band_s, band_r, neighbour)

    def small_ends(d, device):
        if d <= half:
            return device, xor_index(device, d)
        return xor_index(device, half), xor_index(device, d - half)

    def smalls_out(d):
        slot, t = small_ends(d, me)
        first = d <= half
        return (
            remote(wave if first else wave_all.at[slot], wave_all.at[slot], wave_ss.at[d], wave_sr.at[d], t),
            remote(aper if first else aper_all.at[slot], aper_all.at[slot], aper_ss.at[d], aper_sr.at[d], t),
        )

    def smalls_in(d):
        sender = xor_index(me, d if d <= half else d - half)
        slot, _ = small_ends(d, sender)
        return (
            remote(wave_all.at[slot], wave_all.at[slot], wave_ss.at[d], wave_sr.at[d], sender),
            remote(aper_all.at[slot], aper_all.at[slot], aper_ss.at[d], aper_sr.at[d], sender),
        )

    def obl_left():
        return remote(obl.at[:, 0:HALO], obl_win.at[:, HALO + width:HALO + width + HALO], obl_ss.at[0], obl_sr.at[0], me - 1)

    def obl_right():
        return remote(obl.at[:, width - HALO:width], obl_win.at[:, 0:HALO], obl_ss.at[1], obl_sr.at[1], me + 1)

    def own_smalls():
        return (
            pltpu.make_async_copy(wave, wave_all.at[me], loc.at[1]),
            pltpu.make_async_copy(aper, aper_all.at[me], loc.at[2]),
            pltpu.make_async_copy(obl, obl_win.at[:, HALO:HALO + width], loc.at[3]),
        )

    def to_scalar():
        return pltpu.make_async_copy(aper_all, aper_s, loc.at[4])

    barrier = pltpu.get_barrier_semaphore()
    for d in range(1, n):
        pl.semaphore_signal(barrier, inc=1, device_id={"src": xor_index(me, d)},
                            device_id_type=pl.DeviceIdType.MESH)
    pl.semaphore_wait(barrier, n - 1)

    order, items = make_plan(n, inner, parts)
    state = {"started": 0, "done": 0, "ext": set(), "mate": set()}

    def piece_act(piece, sending, act):
        kind, d, h = piece
        if kind == "inner":
            act(inner_out(d, h) if sending else inner_in(d, h))
        elif sending:
            both_ways(direct(xor_index(me, d), d), lambda w: act(base_out(d, h, w)))
        else:
            both_ways(direct(me, d), lambda w: act(base_in(d, h, w)))

    def size(piece):
        return 2 if piece[0] == "near" else 1

    def fill():
        while state["started"] < len(order) and (
                sum(size(p) for p in order[state["done"]:state["started"] + 1]) <= AHEAD):
            piece_act(order[state["started"]], True, lambda copy: copy.start())
            state["started"] += 1

    def pump():
        piece = order[state["done"]]
        piece_act(piece, True, lambda copy: copy.wait_send())
        state["done"] += 1
        fill()
        piece_act(piece, False, lambda copy: copy.wait_recv())
        kind, d, h = piece
        if kind != "inner" and handed(me, d) is not False:
            @pl.when(inside & handed(me, d))
            def _():
                ext_out(d, h).start()
        if d > 1 and (kind != "edge" or not inner):
            mate_out(d, h).start()

    def ready(d, h):
        if d == 0:
            if "own" not in state:
                state["own"] = True
                for part in range(parts):
                    both_ways(jnp.logical_not(edge(me)), lambda w: own_copy(part, w).wait())
            return
        for e in (d + 1, d):
            mate_in(e, h).wait_recv()
        if high_bit(d) >= 4:
            high = high_bit(d)
            group = [e for e in range(high, 2 * high) if (e, h) not in state["ext"]]
            if group:
                @pl.when(inside & handed(me, d))
                def _():
                    for e in group:
                        ext_in(e, h).wait_recv()
                state["ext"] |= {(e, h) for e in group}

    def smalls_ready():
        for d in range(1, n):
            if d != half:
                for copy in smalls_in(d):
                    copy.wait_recv()
        for copy in own_smalls():
            copy.wait()

        @pl.when(me > 0)
        def _():
            obl_right().wait_recv()

        @pl.when(me < n - 1)
        def _():
            obl_left().wait_recv()
        to_scalar().start()
        to_scalar().wait()

    def forward_smalls():
        for copy in smalls_in(half):
            copy.wait_recv()
        for d in range(half + 1, n):
            for copy in smalls_out(d):
                copy.start()

    def make_data(re, im, wave_re, wave_im, factor):
        re, im = re.astype(jnp.float32), im.astype(jnp.float32)
        s_re = (re * wave_re - im * wave_im).astype(jnp.bfloat16).astype(jnp.float32)
        s_im = (re * wave_im + im * wave_re).astype(jnp.bfloat16).astype(jnp.float32)
        return (s_re * factor).astype(jnp.bfloat16), (s_im * factor).astype(jnp.bfloat16)

    def wave_columns(s, row, count):
        part = wave_all[s, :, pl.ds(pl.multiple_of(row, BLK), count)]
        part = jnp.concatenate([part, jnp.zeros((6, count), jnp.float32)])
        part = jnp.transpose(part)
        return part[:, 0:1], part[:, 1:2]

    def build_rhs():
        for b in range(width // HALO + 2):
            g = jnp.clip(me * (width // HALO) - 1 + b, 0, total // HALO - 1)
            outer = b in (0, width // HALO + 1)
            other = odd == (1 if b else 0)
            row = pl.multiple_of(jnp.where(other, me * rows, g * HALO) if outer else g * HALO, HALO)
            wave_re, wave_im = wave_columns(g // (rows // HALO), (g % (rows // HALO)) * HALO, HALO)
            for j in range(cols):
                pair = [k for k in (APW * b, APW * b + 1) if 0 <= k - j < WIN]
                if not pair:
                    continue
                at = slice(HALO + j * BLK, HALO + (j + 1) * BLK)
                re, im = recv[0, pl.ds(row, HALO), at], recv[1, pl.ds(row, HALO), at]
                first = j * BLK - (width - HALO if b else 0)
                if outer and 0 <= first < HALO:
                    re = jnp.where(other, band[0, :, first:first + BLK], re)
                    im = jnp.where(other, band[1, :, first:first + BLK], im)
                b_re, b_im = make_data(re, im, wave_re, wave_im, obl_win[0:1, at])
                for k in pair:
                    part = slice((k - APW * b) * BLK, (k - APW * b + 1) * BLK)
                    top = (k - j) * 2 * BLK
                    rhs[j, top:top + BLK, :BLK] = -b_re[part]
                    rhs[j, top:top + BLK, BLK:] = -b_im[part]
                    rhs[j, top + BLK:top + 2 * BLK, :BLK] = b_im[part]
                    rhs[j, top + BLK:top + 2 * BLK, BLK:] = -b_re[part]

    def multiply(s, h):
        first = pl.multiple_of(s * rows + h * part_rows, BLK)
        here = pl.ds(first, part_rows)
        wave_re, wave_im = wave_columns(s, h * part_rows, part_rows)
        for k in range(cols + 2 * APW):
            at = slice(k * BLK, (k + 1) * BLK)
            d_re, d_im = make_data(recv[0, here, at], recv[1, here, at], wave_re, wave_im, obl_win[0:1, at])
            left[:, 2 * k * BLK:(2 * k + 1) * BLK] = d_re
            left[:, (2 * k + 1) * BLK:(2 * k + 2) * BLK] = d_im
        for j in range(cols):
            strips = []
            for r in range(part_rows // BLK):
                listed = [aper_s[s, h * (part_rows // BLK) + r, t, me * cols + j] for t in range(entries)]
                blocks = []
                for w in range(WIN):
                    k = me * cols + j + w - APW
                    hit = listed[0] == k
                    for entry in listed[1:]:
                        hit = hit | (entry == k)
                    hit = hit & (k >= 0) & (k < block_total)
                    block = left[r * BLK:(r + 1) * BLK, (j + w) * 2 * BLK:(j + w + 1) * 2 * BLK]
                    blocks.append(jnp.where(hit, block, jnp.zeros_like(block)))
                strips.append(jnp.concatenate(blocks, axis=1))
            product = jnp.dot(jnp.concatenate(strips, axis=0), rhs[j], preferred_element_type=jnp.float32)
            out[0, here, j * BLK:(j + 1) * BLK] = product[:, :BLK].astype(jnp.bfloat16)
            out[1, here, j * BLK:(j + 1) * BLK] = product[:, BLK:].astype(jnp.bfloat16)

    @pl.when(banded)
    def _():
        band_out().start()
    fill()
    for h in range(parts):
        both_ways(jnp.logical_not(edge(me)), lambda w: own_copy(h, w).start())
    for d in list(range(half, 0, -1)):
        for copy in smalls_out(d):
            copy.start()

    @pl.when(me > 0)
    def _():
        obl_left().start()

    @pl.when(me < n - 1)
    def _():
        obl_right().start()
    for copy in own_smalls():
        copy.start()
    forward_smalls()

    def item(step, carry):
        for index, (last, d, h) in enumerate(items):
            @pl.when(step == 2 * index)
            def _(last=last, d=d, h=h, index=index):
                upto = len(order) if index == len(items) - 1 else min(last + 1 + SLACK, len(order))
                while state["done"] < upto:
                    pump()
                ready(d, h)
                if index == 0:
                    for other in range(1, parts):
                        if ("near", 0, other) not in state["mate"]:
                            pass
                    smalls_ready()

                    @pl.when(banded)
                    def _():
                        band_in().wait_recv()

                    @pl.when(jnp.logical_not(banded))
                    def _():
                        row = jnp.clip(me * rows - HALO + (rows + HALO) * odd, 0, total - HALO)
                        band[...] = recv[:, pl.ds(pl.multiple_of(row, HALO), HALO), lanes(HALO + (width - HALO) * odd, HALO)]
                    build_rhs()

        q = step // 2
        d = pick(q, [d for _, d, _ in items]) + 1 - step % 2
        multiply(xor_traced(me, d, n), pick(q, [h for _, _, h in items]))
        return carry

    lax.fori_loop(0, 2 * len(items), item, 0)

    for d in range(1, n):
        for copy in smalls_out(d):
            copy.wait_send()
        for h in range(parts):
            if d > 1:
                mate_out(d, h).wait_send()
            if handed(me, d) is not False:
                @pl.when(inside & handed(me, d))
                def _(d=d, h=h):
                    ext_out(d, h).wait_send()

    @pl.when(banded)
    def _():
        band_out().wait_send()

    @pl.when(me > 0)
    def _():
        obl_left().wait_send()

    @pl.when(me < n - 1)
    def _():
        obl_right().wait_send()


def per_device(n, shots, wavelet, obliquity, aperture):
    rows, total = shots.shape[1], shots.shape[2]
    width = total // n
    cols = width // BLK
    half = n // 2
    parts = min(MOST_PARTS, rows // BLK)
    spread = width + 2 * HALO
    aper = jnp.transpose(aperture, (0, 2, 1))
    anywhere = pl.BlockSpec(memory_space=pl.ANY)
    dma = pltpu.SemaphoreType.DMA
    return pl.pallas_call(
        functools.partial(kernel, n, rows, width),
        out_shape=pltpu.VMEM((2, total, width), jnp.bfloat16),
        in_specs=[anywhere] * 4,
        out_specs=pl.BlockSpec(memory_space=pltpu.VMEM),
        scratch_shapes=[
            pltpu.VMEM((2, total, spread), jnp.bfloat16),
            pltpu.VMEM((2, HALO, HALO), jnp.bfloat16),
            pltpu.VMEM((cols, WIN * 2 * BLK, 2 * BLK), jnp.bfloat16),
            pltpu.VMEM((rows // parts, (cols + 2 * APW) * 2 * BLK), jnp.bfloat16),
            pltpu.VMEM((n,) + wavelet.shape, jnp.float32),
            pltpu.VMEM((1, spread), jnp.float32),
            pltpu.VMEM((n,) + aper.shape, jnp.int32),
            pltpu.SMEM((n,) + aper.shape, jnp.int32),
            dma((n * parts,)), dma((n * parts,)), dma((half * parts,)), dma((half * parts,)), dma, dma,
            dma((n * parts,)), dma((n * parts,)), dma(((n - 4) * parts,)), dma(((n - 4) * parts,)),
            dma((n,)), dma((n,)), dma((n,)), dma((n,)), dma((2,)), dma((2,)), dma((5 + parts,)),
        ],
        compiler_params=pltpu.CompilerParams(
            collective_id=0, has_side_effects=True, vmem_limit_bytes=42 * 1024 * 1024),
    )(shots, wavelet, obliquity[None, :], aper)


def solution(mesh):
    return jax.shard_map(
        functools.partial(per_device, mesh.shape["src"]),
        mesh=mesh,
        in_specs=(P("freq", "src", None), P("freq", "src"), P("src"), P("src", None, None)),
        out_specs=P("freq", None, "src"),
        check_vma=False,
    )
```

```python
import functools

import jax
import jax.numpy as jnp
from jax import lax
from jax.experimental import pallas as pl
from jax.experimental.pallas import tpu as pltpu
from jax.sharding import PartitionSpec as P

BLK = 128
APW = 2
WIN = 2 * APW + 1
HALO = APW * BLK
MOST_PARTS = 2
AHEAD = 9
SLACK = 3


def xor_index(index, d):
    bit, result = 1, index
    while bit <= d:
        if d & bit:
            result = result + bit - 2 * bit * ((index // bit) % 2)
        bit *= 2
    return result


def xor_traced(a, b, n):
    bit, result = 1, 0
    while bit < n:
        result = result + bit * ((a // bit + b // bit) % 2)
        bit *= 2
    return result


def pick(index, table):
    result = jnp.int32(0)
    for i, value in enumerate(table):
        result = result + jnp.where(index == i, value, 0)
    return result


def high_bit(d):
    return 1 << (d.bit_length() - 1)


def merge(a, b):
    out, i, j = [], 0, 0
    while i < len(a) or j < len(b):
        if j == len(b) or (i < len(a) and (i + 1) * len(b) <= (j + 1) * len(a)):
            out.append(a[i])
            i += 1
        else:
            out.append(b[j])
            j += 1
    return out


def make_plan(n, inner, parts):
    half = n // 2
    near_pairs = [0] + list(range(half - 2, 1, -2))
    far_pairs = list(range(n - 2, half - 1, -2))

    def pieces(kind, pairs):
        return [(kind, d + 1 - u, h) for d in pairs for h in range(parts) for u in range(2) if d + 1 - u]

    far = pieces("edge", far_pairs) + (pieces("inner", far_pairs) if inner else [])
    near = pieces("near", near_pairs)
    order = near[:parts] + merge(far, near[parts:])
    at = {piece: i for i, piece in enumerate(order)}
    items = []
    for d in near_pairs + far_pairs:
        for h in range(parts):
            if d < half:
                needs = [("near", e, h) for e in (d, d + 1) if e]
                kind = "near"
            else:
                needs = [("edge", e, h) for e in (d, d + 1)]
                needs += [("inner", e, h) for e in (d, d + 1)] if inner else []
                kind = "edge"
            x = 3
            while d and x < high_bit(d):
                needs += [(kind, e ^ x, h) for e in (d, d + 1)]
                x = 2 * x + 1
            if d == 0:
                needs += [("near", 1, e) for e in range(parts)] + [("edge", n - 1, e) for e in range(parts)]
            items.append((max(at[p] for p in needs), d, h))
    items.sort()
    return order, items


def kernel(n, rows, width, shots, wave, obl, aper, out,
           recv, band, rhs, left, wave_all, obl_win, aper_all, aper_s,
           base_s, base_r, in_s, in_r, band_s, band_r, mate_s, mate_r, ext_s, ext_r,
           wave_ss, wave_sr, aper_ss, aper_sr, obl_ss, obl_sr, loc):
    parts = min(MOST_PARTS, rows // BLK)
    me = lax.axis_index("src")
    half = n // 2
    odd = me % 2
    mate = xor_index(me, 1)
    neighbour = me - 1 + 2 * odd
    total = n * rows
    block_total = total // BLK
    cols = width // BLK
    part_rows = rows // parts
    inner = width - HALO
    entries = aper.shape[1]

    def edge(t):
        return (t == 0) | (t == n - 1)

    def middle(t):
        return (t == half - 1) | (t == half)

    inside = jnp.logical_not(edge(me))

    def handed(t, d):
        high = high_bit(d)
        if high < 4:
            return False
        return (t + t % 2) % high != 0

    def direct(t, d):
        if handed(t, d) is False:
            return jnp.logical_not(edge(t))
        return jnp.logical_not(edge(t) | handed(t, d))

    def lanes(col, wide):
        return pl.ds(pl.multiple_of(col, BLK), wide)

    def rows_of(s, col, wide, h):
        return recv.at[:, pl.ds(pl.multiple_of(s * rows + h * part_rows, BLK), part_rows), lanes(col, wide)]

    def cols_of(col, wide, h):
        return shots.at[:, pl.ds(h * part_rows, part_rows), lanes(col, wide)]

    def remote(src, dst, send, got, t):
        return pltpu.make_async_remote_copy(
            src_ref=src, dst_ref=dst, send_sem=send, recv_sem=got,
            device_id={"src": t}, device_id_type=pl.DeviceIdType.MESH)

    def both_ways(cond, act):
        @pl.when(cond)
        def _():
            act(True)

        @pl.when(jnp.logical_not(cond))
        def _():
            act(False)

    def span(t, d, wide_case):
        t_odd = t % 2
        if d <= 1:
            if wide_case:
                return t * width - HALO, 0, width + 2 * HALO
            return t * width - HALO * t_odd, HALO * (1 - t_odd), width + HALO
        if d < half:
            if wide_case:
                return t * width - HALO * (1 - t_odd), HALO * t_odd, width + HALO
            return t * width, HALO, width
        if wide_case:
            return t * width + (width - HALO) * t_odd - HALO * (1 - t_odd), width * t_odd, 2 * HALO
        return t * width + (width - HALO) * t_odd, HALO + (width - HALO) * t_odd, HALO

    def base_out(d, h, wide_case):
        t = xor_index(me, d)
        i = d * parts + h
        src_col, dst_col, wide = span(t, d, wide_case)
        return remote(cols_of(src_col, wide, h), rows_of(me, dst_col, wide, h), base_s.at[i], base_r.at[i], t)

    def base_in(d, h, wide_case):
        s = xor_index(me, d)
        i = d * parts + h
        _, dst_col, wide = span(me, d, wide_case)
        place = rows_of(s, dst_col, wide, h)
        return remote(place, place, base_s.at[i], base_r.at[i], s)

    def own_copy(h, wide_case):
        src_col, dst_col, wide = span(me, 0, wide_case)
        return pltpu.make_async_copy(cols_of(src_col, wide, h), rows_of(me, dst_col, wide, h), loc.at[5 + h])

    def inner_out(d, h):
        t = xor_index(me, d)
        i = (d - half) * parts + h
        return remote(cols_of(t * width + HALO * (1 - t % 2), inner, h), rows_of(me, HALO + HALO * (1 - t % 2), inner, h),
                      in_s.at[i], in_r.at[i], t)

    def inner_in(d, h):
        s = xor_index(me, d)
        i = (d - half) * parts + h
        place = rows_of(s, HALO + HALO * (1 - odd), inner, h)
        return remote(place, place, in_s.at[i], in_r.at[i], s)

    def mate_out(d, h):
        i = d * parts + h
        s = xor_index(me, d)
        return remote(rows_of(s, width * (1 - odd) + HALO * odd, HALO, h), rows_of(s, (HALO + width) * odd, HALO, h),
                      mate_s.at[i], mate_r.at[i], mate)

    def mate_in(d, h):
        i = d * parts + h
        place = rows_of(xor_index(mate, d), (HALO + width) * (1 - odd), HALO, h)
        return remote(place, place, mate_s.at[i], mate_r.at[i], mate)

    def ext_out(d, h):
        i = (d - 4) * parts + h
        s = xor_index(me, d)
        return remote(rows_of(s, HALO * (1 - odd) + width * odd, HALO, h), rows_of(s, (HALO + width) * (1 - odd), HALO, h),
                      ext_s.at[i], ext_r.at[i], neighbour)

    def ext_in(d, h):
        i = (d - 4) * parts + h
        place = rows_of(xor_index(neighbour, d), (HALO + width) * odd, HALO, h)
        return remote(place, place, ext_s.at[i], ext_r.at[i], neighbour)

    banded = jnp.logical_not(edge(me) | middle(me))

    def band_out():
        src = shots.at[:, pl.ds(pl.multiple_of((rows - HALO) * odd, HALO), HALO),
                       lanes(neighbour * width + (width - HALO) * (1 - odd), HALO)]
        return remote(src, band, band_s, band_r, neighbour)

    def band_in():
        return remote(band, band, band_s, band_r, neighbour)

    def small_ends(d, device):
        if d <= half:
            return device, xor_index(device, d)
        return xor_index(device, half), xor_index(device, d - half)

    def smalls_out(d):
        slot, t = small_ends(d, me)
        first = d <= half
        return (
            remote(wave if first else wave_all.at[slot], wave_all.at[slot], wave_ss.at[d], wave_sr.at[d], t),
            remote(aper if first else aper_all.at[slot], aper_all.at[slot], aper_ss.at[d], aper_sr.at[d], t),
        )

    def smalls_in(d):
        sender = xor_index(me, d if d <= half else d - half)
        slot, _ = small_ends(d, sender)
        return (
            remote(wave_all.at[slot], wave_all.at[slot], wave_ss.at[d], wave_sr.at[d], sender),
            remote(aper_all.at[slot], aper_all.at[slot], aper_ss.at[d], aper_sr.at[d], sender),
        )

    def obl_left():
        return remote(obl.at[:, 0:HALO], obl_win.at[:, HALO + width:HALO + width + HALO], obl_ss.at[0], obl_sr.at[0], me - 1)

    def obl_right():
        return remote(obl.at[:, width - HALO:width], obl_win.at[:, 0:HALO], obl_ss.at[1], obl_sr.at[1], me + 1)

    def own_smalls():
        return (
            pltpu.make_async_copy(wave, wave_all.at[me], loc.at[1]),
            pltpu.make_async_copy(aper, aper_all.at[me], loc.at[2]),
            pltpu.make_async_copy(obl, obl_win.at[:, HALO:HALO + width], loc.at[3]),
        )

    def to_scalar():
        return pltpu.make_async_copy(aper_all, aper_s, loc.at[4])

    barrier = pltpu.get_barrier_semaphore()
    for d in range(1, n):
        pl.semaphore_signal(barrier, inc=1, device_id={"src": xor_index(me, d)},
                            device_id_type=pl.DeviceIdType.MESH)
    pl.semaphore_wait(barrier, n - 1)

    order, items = make_plan(n, inner, parts)
    state = {"started": 0, "done": 0, "ext": set(), "mate": set()}

    def piece_act(piece, sending, act):
        kind, d, h = piece
        if kind == "inner":
            act(inner_out(d, h) if sending else inner_in(d, h))
        elif sending:
            both_ways(direct(xor_index(me, d), d), lambda w: act(base_out(d, h, w)))
        else:
            both_ways(direct(me, d), lambda w: act(base_in(d, h, w)))

    def size(piece):
        return 2 if piece[0] == "near" else 1

    def fill():
        while state["started"] < len(order) and (
                sum(size(p) for p in order[state["done"]:state["started"] + 1]) <= AHEAD):
            piece_act(order[state["started"]], True, lambda copy: copy.start())
            state["started"] += 1

    def pump():
        piece = order[state["done"]]
        piece_act(piece, True, lambda copy: copy.wait_send())
        state["done"] += 1
        fill()
        piece_act(piece, False, lambda copy: copy.wait_recv())
        kind, d, h = piece
        if kind != "inner" and handed(me, d) is not False:
            @pl.when(inside & handed(me, d))
            def _():
                ext_out(d, h).start()
        if d > 1 and (kind != "edge" or not inner):
            mate_out(d, h).start()

    def ready(d, h):
        if d == 0:
            if "own" not in state:
                state["own"] = True
                for part in range(parts):
                    both_ways(jnp.logical_not(edge(me)), lambda w: own_copy(part, w).wait())
            return
        for e in (d + 1, d):
            mate_in(e, h).wait_recv()
        if high_bit(d) >= 4:
            high = high_bit(d)
            group = [e for e in range(high, 2 * high) if (e, h) not in state["ext"]]
            if group:
                @pl.when(inside & handed(me, d))
                def _():
                    for e in group:
                        ext_in(e, h).wait_recv()
                state["ext"] |= {(e, h) for e in group}

    def smalls_ready():
        for d in range(1, n):
            if d != half:
                for copy in smalls_in(d):
                    copy.wait_recv()
        for copy in own_smalls():
            copy.wait()

        @pl.when(me > 0)
        def _():
            obl_right().wait_recv()

        @pl.when(me < n - 1)
        def _():
            obl_left().wait_recv()
        to_scalar().start()
        to_scalar().wait()

    def forward_smalls():
        for copy in smalls_in(half):
            copy.wait_recv()
        for d in range(half + 1, n):
            for copy in smalls_out(d):
                copy.start()

    def make_data(re, im, wave_re, wave_im, factor):
        re, im = re.astype(jnp.float32), im.astype(jnp.float32)
        s_re = (re * wave_re - im * wave_im).astype(jnp.bfloat16).astype(jnp.float32)
        s_im = (re * wave_im + im * wave_re).astype(jnp.bfloat16).astype(jnp.float32)
        return (s_re * factor).astype(jnp.bfloat16), (s_im * factor).astype(jnp.bfloat16)

    def wave_columns(s, row, count):
        part = wave_all[s, :, pl.ds(pl.multiple_of(row, BLK), count)]
        part = jnp.concatenate([part, jnp.zeros((6, count), jnp.float32)])
        part = jnp.transpose(part)
        return part[:, 0:1], part[:, 1:2]

    def build_rhs():
        for b in range(width // HALO + 2):
            g = jnp.clip(me * (width // HALO) - 1 + b, 0, total // HALO - 1)
            outer = b in (0, width // HALO + 1)
            other = odd == (1 if b else 0)
            row = pl.multiple_of(jnp.where(other, me * rows, g * HALO) if outer else g * HALO, HALO)
            wave_re, wave_im = wave_columns(g // (rows // HALO), (g % (rows // HALO)) * HALO, HALO)
            for j in range(cols):
                pair = [k for k in (APW * b, APW * b + 1) if 0 <= k - j < WIN]
                if not pair:
                    continue
                at = slice(HALO + j * BLK, HALO + (j + 1) * BLK)
                re, im = recv[0, pl.ds(row, HALO), at], recv[1, pl.ds(row, HALO), at]
                first = j * BLK - (width - HALO if b else 0)
                if outer and 0 <= first < HALO:
                    re = jnp.where(other, band[0, :, first:first + BLK], re)
                    im = jnp.where(other, band[1, :, first:first + BLK], im)
                b_re, b_im = make_data(re, im, wave_re, wave_im, obl_win[0:1, at])
                for k in pair:
                    part = slice((k - APW * b) * BLK, (k - APW * b + 1) * BLK)
                    top = (k - j) * 2 * BLK
                    rhs[j, top:top + BLK, :BLK] = -b_re[part]
                    rhs[j, top:top + BLK, BLK:] = -b_im[part]
                    rhs[j, top + BLK:top + 2 * BLK, :BLK] = b_im[part]
                    rhs[j, top + BLK:top + 2 * BLK, BLK:] = -b_re[part]

    def multiply(s, h):
        first = pl.multiple_of(s * rows + h * part_rows, BLK)
        here = pl.ds(first, part_rows)
        wave_re, wave_im = wave_columns(s, h * part_rows, part_rows)
        for k in range(cols + 2 * APW):
            at = slice(k * BLK, (k + 1) * BLK)
            d_re, d_im = make_data(recv[0, here, at], recv[1, here, at], wave_re, wave_im, obl_win[0:1, at])
            left[:, 2 * k * BLK:(2 * k + 1) * BLK] = d_re
            left[:, (2 * k + 1) * BLK:(2 * k + 2) * BLK] = d_im
        for j in range(cols):
            strips = []
            for r in range(part_rows // BLK):
                listed = [aper_s[s, h * (part_rows // BLK) + r, t, me * cols + j] for t in range(entries)]
                blocks = []
                for w in range(WIN):
                    k = me * cols + j + w - APW
                    hit = listed[0] == k
                    for entry in listed[1:]:
                        hit = hit | (entry == k)
                    hit = hit & (k >= 0) & (k < block_total)
                    block = left[r * BLK:(r + 1) * BLK, (j + w) * 2 * BLK:(j + w + 1) * 2 * BLK]
                    blocks.append(jnp.where(hit, block, jnp.zeros_like(block)))
                strips.append(jnp.concatenate(blocks, axis=1))
            product = jnp.dot(jnp.concatenate(strips, axis=0), rhs[j], preferred_element_type=jnp.float32)
            out[0, here, j * BLK:(j + 1) * BLK] = product[:, :BLK].astype(jnp.bfloat16)
            out[1, here, j * BLK:(j + 1) * BLK] = product[:, BLK:].astype(jnp.bfloat16)

    @pl.when(banded)
    def _():
        band_out().start()
    fill()
    for h in range(parts):
        both_ways(jnp.logical_not(edge(me)), lambda w: own_copy(h, w).start())
    for d in list(range(half, 0, -1)):
        for copy in smalls_out(d):
            copy.start()

    @pl.when(me > 0)
    def _():
        obl_left().start()

    @pl.when(me < n - 1)
    def _():
        obl_right().start()
    for copy in own_smalls():
        copy.start()
    forward_smalls()

    def item(step, carry):
        for index, (last, d, h) in enumerate(items):
            @pl.when(step == 2 * index)
            def _(last=last, d=d, h=h, index=index):
                upto = len(order) if index == len(items) - 1 else min(last + 1 + SLACK, len(order))
                while state["done"] < upto:
                    pump()
                ready(d, h)
                if index == 0:
                    for other in range(1, parts):
                        if ("near", 0, other) not in state["mate"]:
                            pass
                    smalls_ready()

                    @pl.when(banded)
                    def _():
                        band_in().wait_recv()

                    @pl.when(jnp.logical_not(banded))
                    def _():
                        row = jnp.clip(me * rows - HALO + (rows + HALO) * odd, 0, total - HALO)
                        band[...] = recv[:, pl.ds(pl.multiple_of(row, HALO), HALO), lanes(HALO + (width - HALO) * odd, HALO)]
                    build_rhs()

        q = step // 2
        d = pick(q, [d for _, d, _ in items]) + 1 - step % 2
        multiply(xor_traced(me, d, n), pick(q, [h for _, _, h in items]))
        return carry

    lax.fori_loop(0, 2 * len(items), item, 0)

    for d in range(1, n):
        for copy in smalls_out(d):
            copy.wait_send()
        for h in range(parts):
            if d > 1:
                mate_out(d, h).wait_send()
            if handed(me, d) is not False:
                @pl.when(inside & handed(me, d))
                def _(d=d, h=h):
                    ext_out(d, h).wait_send()

    @pl.when(banded)
    def _():
        band_out().wait_send()

    @pl.when(me > 0)
    def _():
        obl_left().wait_send()

    @pl.when(me < n - 1)
    def _():
        obl_right().wait_send()


def per_device(n, shots, wavelet, obliquity, aperture):
    rows, total = shots.shape[1], shots.shape[2]
    width = total // n
    cols = width // BLK
    half = n // 2
    parts = min(MOST_PARTS, rows // BLK)
    spread = width + 2 * HALO
    aper = jnp.transpose(aperture, (0, 2, 1))
    anywhere = pl.BlockSpec(memory_space=pl.ANY)
    dma = pltpu.SemaphoreType.DMA
    return pl.pallas_call(
        functools.partial(kernel, n, rows, width),
        out_shape=pltpu.VMEM((2, total, width), jnp.bfloat16),
        in_specs=[anywhere] * 4,
        out_specs=pl.BlockSpec(memory_space=pltpu.VMEM),
        scratch_shapes=[
            pltpu.VMEM((2, total, spread), jnp.bfloat16),
            pltpu.VMEM((2, HALO, HALO), jnp.bfloat16),
            pltpu.VMEM((cols, WIN * 2 * BLK, 2 * BLK), jnp.bfloat16),
            pltpu.VMEM((rows // parts, (cols + 2 * APW) * 2 * BLK), jnp.bfloat16),
            pltpu.VMEM((n,) + wavelet.shape, jnp.float32),
            pltpu.VMEM((1, spread), jnp.float32),
            pltpu.VMEM((n,) + aper.shape, jnp.int32),
            pltpu.SMEM((n,) + aper.shape, jnp.int32),
            dma((n * parts,)), dma((n * parts,)), dma((half * parts,)), dma((half * parts,)), dma, dma,
            dma((n * parts,)), dma((n * parts,)), dma(((n - 4) * parts,)), dma(((n - 4) * parts,)),
            dma((n,)), dma((n,)), dma((n,)), dma((n,)), dma((2,)), dma((2,)), dma((5 + parts,)),
        ],
        compiler_params=pltpu.CompilerParams(
            collective_id=0, has_side_effects=True, vmem_limit_bytes=42 * 1024 * 1024),
    )(shots, wavelet, obliquity[None, :], aper)


def solution(mesh):
    return jax.shard_map(
        functools.partial(per_device, mesh.shape["src"]),
        mesh=mesh,
        in_specs=(P("freq", "src", None), P("freq", "src"), P("src"), P("src", None, None)),
        out_specs=P("freq", None, "src"),
        check_vma=False,
    )
```
